32 devices in a mesh: groups: 2 (over x), seq: 16 (over z, y, core).
Axes of the slice: x: 2, y: 2, z: 4, core: 2. Of those that a mesh axis runs over, the one named last changes fastest.
Arguments:
- visual: bfloat16 [32768, 1152], P(('groups', 'seq')), parts along dimension 0, may hold values from -18 to 18
- vis_proj: bfloat16 [1152, 1792], replicated, may hold values from -0.1875 to 0.1875
- kv_proj: bfloat16 [1792, 512], replicated, may hold values from -0.125 to 0.125
- out_proj: bfloat16 [1792, 1792], P(None, 'seq'), may hold values from -0.125 to 0.125
- queries: bfloat16 [256, 1792], P(('groups', 'seq')), parts along dimension 0, may hold values from -350 to 350
- frame_range: int32 [2, 2], P('groups'), parts along dimension 0, may hold values from 0 to 64, as said below
- text_lens: int32 [2], P('groups'), parts along dimension 0, may hold values from 1 to 128, as said below
Outputs:
- attended: bfloat16 [256, 1792], P(('groups', 'seq')), parts along dimension 0
The draws below stay inside these ranges and needn't reach their ends.
There are 2 independent parts, one for each index of `groups`. The reference program is written for one: setup_inputs(seed, part) draws one part's arguments, and reference() takes and returns one part's arrays. A program takes and returns all parts, laid end to end along the dimension named above; an argument that names none is the same for every part. Nothing has to cross between parts.
Inputs may be any that keep to these rules, and one draw needn't show every extreme that they name: frame_range[b, 0] < frame_range[b, 1] for every block b; some block attends all 64 frames. `text_lens`: some block is full.
All inputs are finite; a program needn't handle non-finite values.
Results may differ from the reference program's by a relative error of at most 0.02.
The reference program's roundings to bfloat16 on the way (of `hidden`, `key_value`, `weights_low` and `attention`) count: a program that leaves them out, or rounds other values in their place, can miss the bound.
Values may be sent and summed in bfloat16 or wider, within the bound.
A program may use at most 128 MiB of HBM per device.

```python
import jax
import jax.numpy as jnp
from jax import lax

D_VIS = 1152
D_WIN = 1792
HEADS = 14
KV_HEADS = 2
HEAD_DIM = 128
OUT_WIN = 1792
FRAME_TOK = 256
QBLK = 128
VIS = 16384
TEXT = 128
FRAMES = 64
QBLOCKS = 1


def draw_visual(key, part):
    key_rows, key_vals = jax.random.split(key, 2)
    scales = jnp.exp(jax.random.uniform(key_rows, (VIS, 1), jnp.float32, jnp.log(0.3), jnp.log(3.0)))
    base = jnp.clip(jax.random.normal(key_vals, (VIS, D_VIS), jnp.float32), -6.0, 6.0)
    return (base * scales).astype(jnp.bfloat16)


def draw_queries(key, part):
    key_rows, key_vals = jax.random.split(key, 2)
    width_all = HEADS * HEAD_DIM
    scales = jnp.exp(jax.random.uniform(key_rows, (TEXT, 1), jnp.float32, jnp.log(0.5), jnp.log(5.0)))
    base = jnp.clip(jax.random.normal(key_vals, (TEXT, width_all), jnp.float32), -6.0, 6.0)
    return (base * scales).astype(jnp.bfloat16)


def draw_frame_range(key, part):
    key_span, key_start, key_full = jax.random.split(key, 3)
    spans = jax.random.randint(key_span, (QBLOCKS,), 1, FRAMES + 1)
    starts = jax.random.randint(key_start, (QBLOCKS,), 0, FRAMES - spans + 1)
    full_block = jax.random.randint(key_full, (), 0, QBLOCKS)
    chosen = jnp.arange(QBLOCKS, dtype=jnp.int32) == full_block
    lower = jnp.where(chosen, 0, starts)
    upper = jnp.where(chosen, FRAMES, starts + spans)
    return jnp.stack([lower, upper], axis=1).astype(jnp.int32)


def draw_text_lens(key, part):
    key_len, key_full = jax.random.split(key, 2)
    lengths = jax.random.randint(key_len, (QBLOCKS,), 1, QBLK + 1)
    full_block = jax.random.randint(key_full, (), 0, QBLOCKS)
    chosen = jnp.arange(QBLOCKS, dtype=jnp.int32) == full_block
    return jnp.where(chosen, QBLK, lengths).astype(jnp.int32)


def levels(key, extent, cuts, smallest, top_value):
    def one(axis_at, parts):
        heights = jax.random.uniform(jax.random.fold_in(jax.random.fold_in(key, 6), axis_at), (parts,), jnp.float32, smallest / len(cuts), top_value / len(cuts))
        return jnp.repeat(jnp.exp(heights), extent[axis_at] // parts).reshape((-1,) + (1,) * (len(extent) - axis_at - 1))

    factor_of = one(*cuts[0])
    for cut in cuts[1:]:
        factor_of = factor_of * one(*cut)
    return factor_of


def normal_values(rng, extent, scale, limit, pieces=(), kind=jnp.bfloat16):
    drawn = scale * jax.random.normal(rng, extent, jnp.float32)
    if pieces:
        drawn = drawn * levels(rng, extent, pieces, -0.22, 0.18)
    return jnp.clip(drawn, -limit, limit).astype(kind)


def setup_inputs(seed: int = 0, part: int = 0) -> dict:
    key_of = jax.random.split(jax.random.key(seed), 8)
    own_keys = jax.random.split(jax.random.fold_in(key_of[7], part), 8)
    visual = draw_visual(jax.random.fold_in(jax.random.fold_in(key_of[7], part), 71), part)
    vis_proj = normal_values(key_of[1], (D_VIS, D_WIN), D_VIS ** -0.5, 0.1875)
    kv_proj = normal_values(key_of[2], (D_WIN, 2 * KV_HEADS * HEAD_DIM), D_WIN ** -0.5, 0.125)
    out_proj = normal_values(key_of[3], (HEADS * HEAD_DIM, OUT_WIN), (HEADS * HEAD_DIM) ** -0.5, 0.125, ((1, 16),))
    queries = draw_queries(jax.random.fold_in(jax.random.fold_in(key_of[7], part), 71), part)
    frame_range = draw_frame_range(jax.random.fold_in(jax.random.fold_in(key_of[7], part), 71), part)
    text_lens = draw_text_lens(jax.random.fold_in(jax.random.fold_in(key_of[7], part), 71), part)
    return dict(visual=visual, vis_proj=vis_proj, kv_proj=kv_proj, out_proj=out_proj, queries=queries, frame_range=frame_range, text_lens=text_lens)


def reference(visual, vis_proj, kv_proj, out_proj, queries, frame_range, text_lens):
    hidden = jax.nn.gelu(jnp.dot(visual, vis_proj, preferred_element_type=jnp.float32), approximate=True).astype(jnp.bfloat16)
    key_value = jnp.dot(hidden, kv_proj, preferred_element_type=jnp.float32).astype(jnp.bfloat16)
    kv_width = KV_HEADS * HEAD_DIM
    key_rows = key_value[:, :kv_width].reshape(VIS, KV_HEADS, HEAD_DIM).astype(jnp.float32)
    value_rows = key_value[:, kv_width:].reshape(VIS, KV_HEADS, HEAD_DIM).astype(jnp.float32)
    frames = jnp.arange(VIS, dtype=jnp.int32) // FRAME_TOK
    group_size = HEADS // KV_HEADS
    stacked = queries.reshape(QBLOCKS, QBLK, KV_HEADS, group_size, HEAD_DIM)
    positions = jnp.arange(QBLK, dtype=jnp.int32)

    def one_block(packed):
        query_rows, bounds, length = packed
        allowed = (frames >= bounds[0]) & (frames < bounds[1])
        scores = jnp.einsum('tkgd,rkd->tkgr', query_rows.astype(jnp.float32), key_rows) * (HEAD_DIM ** -0.5)
        masked = jnp.where(allowed, scores, -jnp.inf)
        maxima = jnp.max(masked, axis=-1, keepdims=True)
        weights = jnp.where(allowed, jnp.exp(masked - maxima), 0.0)
        totals = jnp.sum(weights, axis=-1)
        weights_low = lax.optimization_barrier(weights.astype(jnp.bfloat16)).astype(jnp.float32)
        numer = jnp.einsum('tkgr,rkd->tkgd', weights_low, value_rows)
        result = numer / totals[..., None]
        valid_rows = positions < length
        result = jnp.where(valid_rows[:, None, None, None], result, 0.0)
        return result.reshape(QBLK, HEADS * HEAD_DIM).astype(jnp.bfloat16)

    attention = lax.map(one_block, (stacked, frame_range, text_lens)).reshape(TEXT, HEADS * HEAD_DIM)
    return jnp.dot(attention, out_proj, preferred_element_type=jnp.float32).astype(jnp.bfloat16)
```

```python
import functools
import math

import jax
import jax.numpy as jnp
from jax import lax
from jax.experimental import pallas as pl
from jax.experimental.pallas import tpu as pltpu
from jax.sharding import PartitionSpec as P

HEADS = 14
KV_HEADS = 2
GROUP = HEADS // KV_HEADS
HEAD_DIM = 128
FRAME_TOK = 256
QBLK = 128
HALF = GROUP * HEAD_DIM
INNER = 4
COLS = 256
ROWS = 256
NEG = -1e30
FLOOR = -1e29
EXP_SCALE = HEAD_DIM ** (-0.5) * math.log2(math.e)
GELU_SCALE = math.sqrt(2.0 / math.pi)
MESH = pl.DeviceIdType.MESH


def gelu(v):
    return 0.5 * v * (1.0 + jnp.tanh(GELU_SCALE * (v + 0.044715 * (v * v * v))))


def kernel(
    n,
    vis_hbm,
    vp_hbm,
    kvp_hbm,
    wo_hbm,
    q_ref,
    range_ref,
    lens_ref,
    out_ref,
    vis,
    vp,
    kvp,
    wbuf,
    hidden,
    kvbuf,
    kvsend,
    qbuf,
    nums,
    numrecv,
    stats,
    statrecv,
    attn,
    yb,
    yrecv,
    load_sem,
    vp_sem,
    w_send,
    w_recv,
    kv_send,
    kv_recv,
    q_send,
    q_recv,
    n_send,
    n_recv,
    s_send,
    s_recv,
    a_send,
    a_recv,
    y_send,
    y_recv,
):
    me = lax.axis_index("seq")
    core = lax.rem(me, 2)
    other = 1 - core
    sibling = me + 1 - 2 * core
    inner = lax.rem(me, INNER)
    outer = lax.div(me, INNER)
    base = me - inner
    across_slot = lax.rem(inner + 2, INNER)
    across = base + across_slot
    sibling_slot = sibling - base
    last_slot = lax.rem(sibling_slot + 2, INNER)
    outers = n // INNER
    own = q_ref.shape[0]
    local = vis.shape[0]
    width = vp.shape[1]
    chunks = width // COLS
    blocks = n * own // QBLK
    per_block = QBLK // own

    vis_copy = pltpu.make_async_copy(vis_hbm, vis, load_sem.at[0])
    vis_copy.start()

    def vp_copy(j):
        cols = pl.ds(pl.multiple_of(j * COLS, COLS), COLS)
        return pltpu.make_async_copy(vp_hbm.at[:, cols], vp.at[:, cols], vp_sem.at[j])

    vp_copy(0).start()
    w_copy = pltpu.make_async_copy(wo_hbm, wbuf.at[inner], load_sem.at[1])
    w_copy.start()
    for j in range(1, chunks):
        vp_copy(j).start()
    kvp_copy = pltpu.make_async_copy(kvp_hbm, kvp, load_sem.at[2])
    kvp_copy.start()

    barrier = pltpu.get_barrier_semaphore()

    @pl.loop(1, n)
    def _(i):
        pl.semaphore_signal(
            barrier, inc=1, device_id={"seq": lax.rem(me + i, n)}, device_id_type=MESH
        )

    def remote(src, dst, send, recv, peer):
        return pltpu.make_async_remote_copy(
            src_ref=src,
            dst_ref=dst,
            send_sem=send,
            recv_sem=recv,
            device_id={"seq": peer},
            device_id_type=MESH,
        )

    def hidden_chunk(j):
        vp_copy(j).wait()
        cols = pl.ds(pl.multiple_of(j * COLS, COLS), COLS)
        for r in range(local // ROWS):
            rows = pl.ds(r * ROWS, ROWS)
            value = jnp.dot(vis[rows, :], vp[:, cols], preferred_element_type=jnp.float32)
            hidden[rows, cols] = gelu(value).astype(jnp.bfloat16)

    vis_copy.wait()
    hidden_chunk(0)

    pl.semaphore_wait(barrier, n - 1)

    def q_copy(peer, slot, index):
        head = pl.ds(pl.multiple_of(lax.rem(peer, 2) * HALF, HEAD_DIM), HALF)
        return remote(q_ref.at[:, head], qbuf.at[slot], q_send.at[index], q_recv.at[slot], peer)

    @pl.loop(1, n)
    def _(i):
        q_copy(lax.rem(me + i, n), me, i).start()

    w_copy.wait()
    w_across = remote(
        wbuf.at[inner], wbuf.at[inner], w_send.at[0], w_recv.at[inner], across
    )
    w_sibling = remote(
        wbuf.at[inner], wbuf.at[inner], w_send.at[1], w_recv.at[inner], sibling
    )
    w_across.start()
    w_sibling.start()
    qbuf[me] = q_ref[:, pl.ds(pl.multiple_of(core * HALF, HEAD_DIM), HALF)]

    @pl.loop(1, chunks)
    def _(j):
        hidden_chunk(j)

    kvp_copy.wait()

    def project(head, store):
        keys = pl.ds(pl.multiple_of(head * HEAD_DIM, HEAD_DIM), HEAD_DIM)
        values = pl.ds(
            pl.multiple_of((KV_HEADS + head) * HEAD_DIM, HEAD_DIM), HEAD_DIM
        )
        weights = jnp.concatenate([kvp[:, keys], kvp[:, values]], axis=1)
        for r in range(local // ROWS):
            rows = pl.ds(r * ROWS, ROWS)
            both = jnp.dot(
                hidden[rows, :], weights, preferred_element_type=jnp.float32
            ).astype(jnp.bfloat16)
            store(rows, both[:, :HEAD_DIM], both[:, HEAD_DIM:])

    def store_send(rows, keys, values):
        kvsend[0, rows, :] = keys
        kvsend[1, rows, :] = values

    def store_own(rows, keys, values):
        kvbuf[0, 0, rows, :] = keys
        kvbuf[0, 1, rows, :] = values

    project(other, store_send)
    kv_copy = remote(kvsend, kvbuf.at[1], kv_send, kv_recv, sibling)
    kv_copy.start()
    project(core, store_own)

    def w_arrival(slot):
        return remote(wbuf.at[slot], wbuf.at[slot], w_send.at[2], w_recv.at[slot], sibling)

    w_arrival(across_slot).wait_recv()
    w_forward = w_arrival(across_slot)
    w_forward.start()

    @pl.loop(1, n)
    def _(i):
        peer = lax.rem(me + i, n)
        q_copy(peer, peer, i).wait_recv()

    kv_copy.wait_recv()

    lane = lax.broadcasted_iota(jnp.int32, (QBLK, HEAD_DIM), 1)
    token = lax.broadcasted_iota(jnp.int32, (1, local), 1)
    for b in range(blocks):
        owners = pl.ds(b * per_block, per_block)
        low = range_ref[b, 0] * FRAME_TOK
        high = range_ref[b, 1] * FRAME_TOK
        allowed = []
        for device in (me, sibling):
            row = token + device * local
            allowed.append((row >= low) & (row < high))
        stat = jnp.zeros((QBLK, HEAD_DIM), jnp.float32)
        for h in range(GROUP):
            cols = pl.ds(h * HEAD_DIM, HEAD_DIM)
            query = (
                qbuf[owners, :, cols]
                .astype(jnp.float32)
                .reshape(QBLK, HEAD_DIM)
                .astype(jnp.bfloat16)
            )
            scores = []
            for slot in range(2):
                raw = lax.dot_general(
                    query,
                    kvbuf[slot, 0],
                    (((1,), (1,)), ((), ())),
                    preferred_element_type=jnp.float32,
                )
                scores.append(jnp.where(allowed[slot], raw, NEG))
            top = jnp.maximum(
                jnp.max(jnp.maximum(scores[0], scores[1]), axis=1, keepdims=True), FLOOR
            )
            weights = [jnp.exp2((s - top) * EXP_SCALE) for s in scores]
            total = jnp.sum(weights[0] + weights[1], axis=1, keepdims=True)
            numer = jnp.dot(
                weights[0].astype(jnp.bfloat16),
                kvbuf[0, 1],
                preferred_element_type=jnp.float32,
            ) + jnp.dot(
                weights[1].astype(jnp.bfloat16),
                kvbuf[1, 1],
                preferred_element_type=jnp.float32,
            )
            nums[owners, :, cols] = numer.reshape(per_block, own, HEAD_DIM).astype(
                jnp.bfloat16
            )
            stat = jnp.where(lane == h, top, stat)
            stat = jnp.where(lane == h + HEAD_DIM // 2, total, stat)
        stats[owners] = stat.reshape(per_block, own, HEAD_DIM)

    def n_copy(row_owner, slot, peer, index):
        return remote(
            nums.at[row_owner], numrecv.at[slot], n_send.at[index], n_recv.at[slot], peer
        )

    def s_copy(row_owner, slot, peer, index):
        return remote(
            stats.at[row_owner], statrecv.at[slot], s_send.at[index], s_recv.at[slot], peer
        )

    @pl.loop(1, n)
    def _(i):
        peer = lax.rem(me + i, n)
        s_copy(peer, me, peer, i).start()
        n_copy(peer, me, peer, i).start()

    numrecv[me] = nums[me]
    statrecv[me] = stats[me]

    @pl.loop(1, n)
    def _(i):
        peer = lax.rem(me + i, n)
        s_copy(peer, peer, peer, i).wait_recv()
        n_copy(peer, peer, peer, i).wait_recv()

    length = lens_ref[lax.div(me * own, QBLK)]
    position = lax.rem(me * own, QBLK) + lax.broadcasted_iota(jnp.int32, (own, HEAD_DIM), 0)
    valid = position < length
    for k in range(KV_HEADS):
        sources = range(k, n, KV_HEADS)
        top = functools.reduce(jnp.maximum, [statrecv[s] for s in sources])
        factors = [jnp.exp2((statrecv[s] - top) * EXP_SCALE) for s in sources]
        totals = functools.reduce(
            jnp.add,
            [
                f * pltpu.roll(statrecv[s], HEAD_DIM // 2, 1)
                for f, s in zip(factors, sources)
            ],
        )
        for h in range(GROUP):
            cols = pl.ds(h * HEAD_DIM, HEAD_DIM)
            sums = functools.reduce(
                jnp.add,
                [
                    numrecv[s, :, cols].astype(jnp.float32) * f[:, h : h + 1]
                    for f, s in zip(factors, sources)
                ],
            )
            normed = jnp.where(valid, sums / totals[:, h : h + 1], 0.0)
            attn[outer, :, pl.ds(k * HALF + h * HEAD_DIM, HEAD_DIM)] = normed.astype(
                jnp.bfloat16
            )

    def a_copy(slot, peer_outer, index):
        return remote(
            attn.at[slot],
            attn.at[slot],
            a_send.at[index],
            a_recv.at[slot],
            peer_outer * INNER + inner,
        )

    for i in range(1, outers):
        a_copy(outer, lax.rem(outer + i, outers), i).start()
    w_arrival(sibling_slot).wait_recv()
    w_arrival(last_slot).wait_recv()
    for i in range(1, outers):
        peer_outer = lax.rem(outer + i, outers)
        a_copy(peer_outer, peer_outer, i).wait_recv()

    rows = (
        attn[...]
        .astype(jnp.float32)
        .reshape(outers * own, HEADS * HEAD_DIM)
        .astype(jnp.bfloat16)
    )
    for j in range(INNER):
        product = jnp.dot(rows, wbuf[j], preferred_element_type=jnp.float32)
        yb[:, j] = product.reshape(outers, own, product.shape[1]).astype(jnp.bfloat16)

    def y_copy(row_outer, slot, peer_outer, index):
        return remote(
            yb.at[row_outer],
            yrecv.at[slot],
            y_send.at[index],
            y_recv.at[slot],
            peer_outer * INNER + inner,
        )

    for i in range(1, outers):
        peer_outer = lax.rem(outer + i, outers)
        y_copy(peer_outer, outer, peer_outer, i).start()
    yrecv[outer] = yb[outer]

    w_across.wait_send()
    w_sibling.wait_send()
    w_forward.wait_send()
    kv_copy.wait_send()

    @pl.loop(1, n)
    def _(i):
        peer = lax.rem(me + i, n)
        q_copy(peer, me, i).wait_send()
        s_copy(peer, me, peer, i).wait_send()
        n_copy(peer, me, peer, i).wait_send()

    for i in range(1, outers):
        peer_outer = lax.rem(outer + i, outers)
        a_copy(outer, peer_outer, i).wait_send()
        y_copy(peer_outer, peer_outer, peer_outer, i).wait_recv()
    for i in range(1, outers):
        peer_outer = lax.rem(outer + i, outers)
        y_copy(peer_outer, outer, peer_outer, i).wait_send()
    out_ref[...] = yrecv[...]


def body(visual, vis_proj, kv_proj, out_proj, queries, frame_range, text_lens):
    n = lax.axis_size("seq")
    own = queries.shape[0]
    local = visual.shape[0]
    outers = n // INNER
    cols = out_proj.shape[1]
    low = jnp.bfloat16
    dma = pltpu.SemaphoreType.DMA
    hbm = pl.BlockSpec(memory_space=pl.ANY)
    smem = pl.BlockSpec(memory_space=pltpu.SMEM)
    vmem = pl.BlockSpec(memory_space=pltpu.VMEM)
    result = pl.pallas_call(
        functools.partial(kernel, n),
        out_shape=jax.ShapeDtypeStruct((outers, INNER, own, cols), low),
        in_specs=[hbm, hbm, hbm, hbm, vmem, smem, smem],
        out_specs=vmem,
        scratch_shapes=[
            pltpu.VMEM(visual.shape, low),
            pltpu.VMEM(vis_proj.shape, low),
            pltpu.VMEM(kv_proj.shape, low),
            pltpu.VMEM((INNER,) + out_proj.shape, low),
            pltpu.VMEM((local, vis_proj.shape[1]), low),
            pltpu.VMEM((2, 2, local, HEAD_DIM), low),
            pltpu.VMEM((2, local, HEAD_DIM), low),
            pltpu.VMEM((n, own, HALF), low),
            pltpu.VMEM((n, own, HALF), low),
            pltpu.VMEM((n, own, HALF), low),
            pltpu.VMEM((n, own, HEAD_DIM), jnp.float32),
            pltpu.VMEM((n, own, HEAD_DIM), jnp.float32),
            pltpu.VMEM((outers, own, HEADS * HEAD_DIM), low),
            pltpu.VMEM((outers, INNER, own, cols), low),
            pltpu.VMEM((outers, INNER, own, cols), low),
            dma((3,)),
            dma((vis_proj.shape[1] // COLS,)),
            dma((3,)),
            dma((INNER,)),
            dma,
            dma,
            dma((n,)),
            dma((n,)),
            dma((n,)),
            dma((n,)),
            dma((n,)),
            dma((n,)),
            dma((outers,)),
            dma((outers,)),
            dma((outers,)),
            dma((outers,)),
        ],
        compiler_params=pltpu.CompilerParams(
            collective_id=0, has_side_effects=True, vmem_limit_bytes=56 * 1024 * 1024
        ),
        name="layer",
    )(visual, vis_proj, kv_proj, out_proj, queries, frame_range, text_lens)
    return jnp.transpose(result.reshape(n, own, cols), (1, 0, 2)).reshape(own, n * cols)


def solution(mesh):
    placed = (
        P(("groups", "seq"), None),
        P(),
        P(),
        P(None, "seq"),
        P(("groups", "seq"), None),
        P("groups", None),
        P("groups"),
    )
    return jax.shard_map(
        body, mesh=mesh, in_specs=placed, out_specs=P(("groups", "seq"), None), check_vma=False
    )
```

```python
import functools
import math

import jax
import jax.numpy as jnp
from jax import lax
from jax.experimental import pallas as pl
from jax.experimental.pallas import tpu as pltpu
from jax.sharding import PartitionSpec as P

HEADS = 14
KV_HEADS = 2
GROUP = HEADS // KV_HEADS
HEAD_DIM = 128
FRAME_TOK = 256
QBLK = 128
HALF = GROUP * HEAD_DIM
INNER = 4
COLS = 256
ROWS = 256
NEG = -1e30
FLOOR = -1e29
EXP_SCALE = HEAD_DIM ** (-0.5) * math.log2(math.e)
GELU_SCALE = math.sqrt(2.0 / math.pi)
GELU_CUBE = 0.044715 * GELU_SCALE
SPLIT = 4
MESH = pl.DeviceIdType.MESH


def gelu(v):
    half = 0.5 * v
    return half + half * jnp.tanh(v * (GELU_SCALE + GELU_CUBE * (v * v)))


def kernel(
    n,
    vis_hbm,
    vp_hbm,
    kvp_hbm,
    wo_hbm,
    q_ref,
    range_ref,
    lens_ref,
    out_ref,
    vis,
    vp,
    kvp,
    wbuf,
    hidden,
    kvbuf,
    kvsend,
    qbuf,
    nums,
    numrecv,
    stats,
    statrecv,
    attn,
    yb,
    yrecv,
    load_sem,
    vp_sem,
    w_send,
    w_recv,
    kv_send,
    kv_recv,
    q_send,
    q_recv,
    n_send,
    n_recv,
    s_send,
    s_recv,
    a_send,
    a_recv,
    y_send,
    y_recv,
):
    me = lax.axis_index("seq")
    core = lax.rem(me, 2)
    other = 1 - core
    sibling = me + 1 - 2 * core
    inner = lax.rem(me, INNER)
    outer = lax.div(me, INNER)
    base = me - inner
    across_slot = lax.rem(inner + 2, INNER)
    across = base + across_slot
    sibling_slot = sibling - base
    last_slot = lax.rem(sibling_slot + 2, INNER)
    outers = n // INNER
    own = q_ref.shape[0]
    local = vis.shape[0]
    width = vp.shape[1]
    chunks = width // COLS
    blocks = n * own // QBLK
    per_block = QBLK // own

    vis_copy = pltpu.make_async_copy(vis_hbm, vis, load_sem.at[0])
    vis_copy.start()

    def vp_copy(j):
        cols = pl.ds(pl.multiple_of(j * COLS, COLS), COLS)
        return pltpu.make_async_copy(vp_hbm.at[:, cols], vp.at[:, cols], vp_sem.at[j])

    vp_copy(0).start()
    w_copy = pltpu.make_async_copy(wo_hbm, wbuf.at[inner], load_sem.at[1])
    w_copy.start()
    for j in range(1, chunks):
        vp_copy(j).start()
    kvp_copy = pltpu.make_async_copy(kvp_hbm, kvp, load_sem.at[2])
    kvp_copy.start()

    barrier = pltpu.get_barrier_semaphore()

    @pl.loop(1, n)
    def _(i):
        pl.semaphore_signal(
            barrier, inc=1, device_id={"seq": lax.rem(me + i, n)}, device_id_type=MESH
        )

    def remote(src, dst, send, recv, peer):
        return pltpu.make_async_remote_copy(
            src_ref=src,
            dst_ref=dst,
            send_sem=send,
            recv_sem=recv,
            device_id={"seq": peer},
            device_id_type=MESH,
        )

    def hidden_chunk(j):
        vp_copy(j).wait()
        cols = pl.ds(pl.multiple_of(j * COLS, COLS), COLS)
        for r in range(local // ROWS):
            rows = pl.ds(r * ROWS, ROWS)
            value = jnp.dot(vis[rows, :], vp[:, cols], preferred_element_type=jnp.float32)
            hidden[rows, cols] = gelu(value).astype(jnp.bfloat16)

    vis_copy.wait()
    hidden_chunk(0)

    pl.semaphore_wait(barrier, n - 1)

    def q_copy(peer, slot, index):
        head = pl.ds(pl.multiple_of(lax.rem(peer, 2) * HALF, HEAD_DIM), HALF)
        return remote(q_ref.at[:, head], qbuf.at[slot], q_send.at[index], q_recv.at[slot], peer)

    @pl.loop(1, n)
    def _(i):
        q_copy(lax.rem(me + i, n), me, i).start()

    w_copy.wait()
    w_across = remote(
        wbuf.at[inner], wbuf.at[inner], w_send.at[0], w_recv.at[inner], across
    )
    w_sibling = remote(
        wbuf.at[inner], wbuf.at[inner], w_send.at[1], w_recv.at[inner], sibling
    )
    w_across.start()
    w_sibling.start()
    qbuf[me] = q_ref[:, pl.ds(pl.multiple_of(core * HALF, HEAD_DIM), HALF)]

    @pl.loop(1, chunks)
    def _(j):
        hidden_chunk(j)

    kvp_copy.wait()

    def project(head, store):
        keys = pl.ds(pl.multiple_of(head * HEAD_DIM, HEAD_DIM), HEAD_DIM)
        values = pl.ds(
            pl.multiple_of((KV_HEADS + head) * HEAD_DIM, HEAD_DIM), HEAD_DIM
        )
        weights = jnp.concatenate([kvp[:, keys], kvp[:, values]], axis=1)
        for r in range(local // ROWS):
            rows = pl.ds(r * ROWS, ROWS)
            both = jnp.dot(
                hidden[rows, :], weights, preferred_element_type=jnp.float32
            ).astype(jnp.bfloat16)
            store(rows, both[:, :HEAD_DIM], both[:, HEAD_DIM:])

    def store_send(rows, keys, values):
        kvsend[0, rows, :] = keys
        kvsend[1, rows, :] = values

    def store_own(rows, keys, values):
        kvbuf[0, 0, rows, :] = keys
        kvbuf[0, 1, rows, :] = values

    project(other, store_send)
    kv_copy = remote(kvsend, kvbuf.at[1], kv_send, kv_recv, sibling)
    kv_copy.start()
    project(core, store_own)

    def w_arrival(slot):
        return remote(wbuf.at[slot], wbuf.at[slot], w_send.at[2], w_recv.at[slot], sibling)

    @pl.loop(1, n)
    def _(i):
        peer = lax.rem(me + i, n)
        q_copy(peer, peer, i).wait_recv()

    kv_copy.wait_recv()

    lane = lax.broadcasted_iota(jnp.int32, (QBLK, HEAD_DIM), 1)
    token = lax.broadcasted_iota(jnp.int32, (1, local), 1)
    def n_copy(row_owner, slot, peer, index, part):
        cols = pl.ds(0, SPLIT * HEAD_DIM) if part == 0 else pl.ds(SPLIT * HEAD_DIM, HALF - SPLIT * HEAD_DIM)
        return remote(
            nums.at[row_owner, :, cols],
            numrecv.at[slot, :, cols],
            n_send.at[part, index],
            n_recv.at[part, slot],
            peer,
        )

    def s_copy(row_owner, slot, peer, index):
        return remote(
            stats.at[row_owner], statrecv.at[slot], s_send.at[index], s_recv.at[slot], peer
        )

    allowed = []
    for b in range(blocks):
        low = range_ref[b, 0] * FRAME_TOK
        high = range_ref[b, 1] * FRAME_TOK
        for device in (me, sibling):
            row = token + device * local
            allowed.append((row >= low) & (row < high))
    stat = [jnp.zeros((QBLK, HEAD_DIM), jnp.float32)] * blocks
    for h in range(GROUP):
        cols = pl.ds(h * HEAD_DIM, HEAD_DIM)
        for b in range(blocks):
            owners = pl.ds(b * per_block, per_block)
            query = (
                qbuf[owners, :, cols]
                .astype(jnp.float32)
                .reshape(QBLK, HEAD_DIM)
                .astype(jnp.bfloat16)
            )
            scores = []
            for slot in range(2):
                raw = lax.dot_general(
                    query,
                    kvbuf[slot, 0],
                    (((1,), (1,)), ((), ())),
                    preferred_element_type=jnp.float32,
                )
                scores.append(jnp.where(allowed[2 * b + slot], raw, NEG))
            top = jnp.maximum(
                jnp.max(jnp.maximum(scores[0], scores[1]), axis=1, keepdims=True), FLOOR
            )
            weights = [jnp.exp2((s - top) * EXP_SCALE) for s in scores]
            total = jnp.sum(weights[0] + weights[1], axis=1, keepdims=True)
            numer = jnp.dot(
                weights[0].astype(jnp.bfloat16),
                kvbuf[0, 1],
                preferred_element_type=jnp.float32,
            ) + jnp.dot(
                weights[1].astype(jnp.bfloat16),
                kvbuf[1, 1],
                preferred_element_type=jnp.float32,
            )
            nums[owners, :, cols] = numer.reshape(per_block, own, HEAD_DIM).astype(
                jnp.bfloat16
            )
            stat[b] = jnp.where(lane == h, top, stat[b])
            stat[b] = jnp.where(lane == h + HEAD_DIM // 2, total, stat[b])
        if h == SPLIT - 1:

            @pl.loop(1, n)
            def _(i):
                peer = lax.rem(me + i, n)
                n_copy(peer, me, peer, i, 0).start()

    for b in range(blocks):
        stats[pl.ds(b * per_block, per_block)] = stat[b].reshape(per_block, own, HEAD_DIM)

    @pl.loop(1, n)
    def _(i):
        peer = lax.rem(me + i, n)
        s_copy(peer, me, peer, i).start()
        n_copy(peer, me, peer, i, 1).start()

    w_arrival(across_slot).wait_recv()
    w_forward = w_arrival(across_slot)
    w_forward.start()

    numrecv[me] = nums[me]
    statrecv[me] = stats[me]

    @pl.loop(1, n)
    def _(i):
        peer = lax.rem(me + i, n)
        s_copy(peer, peer, peer, i).wait_recv()
        n_copy(peer, peer, peer, i, 0).wait_recv()
        n_copy(peer, peer, peer, i, 1).wait_recv()

    length = lens_ref[lax.div(me * own, QBLK)]
    position = lax.rem(me * own, QBLK) + lax.broadcasted_iota(jnp.int32, (own, HEAD_DIM), 0)
    valid = position < length
    def a_copy(slot, peer_outer, index, part):
        cols = pl.ds(part * HALF, HALF)
        return remote(
            attn.at[slot, :, cols],
            attn.at[slot, :, cols],
            a_send.at[part, index],
            a_recv.at[part, slot],
            peer_outer * INNER + inner,
        )

    for k in range(KV_HEADS):
        sources = range(k, n, KV_HEADS)
        top = functools.reduce(jnp.maximum, [statrecv[s] for s in sources])
        factors = [jnp.exp2((statrecv[s] - top) * EXP_SCALE) for s in sources]
        totals = functools.reduce(
            jnp.add,
            [
                f * pltpu.roll(statrecv[s], HEAD_DIM // 2, 1)
                for f, s in zip(factors, sources)
            ],
        )
        for h in range(GROUP):
            cols = pl.ds(h * HEAD_DIM, HEAD_DIM)
            sums = functools.reduce(
                jnp.add,
                [
                    numrecv[s, :, cols].astype(jnp.float32) * f[:, h : h + 1]
                    for f, s in zip(factors, sources)
                ],
            )
            normed = jnp.where(valid, sums / totals[:, h : h + 1], 0.0)
            attn[outer, :, pl.ds(k * HALF + h * HEAD_DIM, HEAD_DIM)] = normed.astype(
                jnp.bfloat16
            )
        for i in range(1, outers):
            a_copy(outer, lax.rem(outer + i, outers), i, k).start()

    w_arrival(sibling_slot).wait_recv()
    w_arrival(last_slot).wait_recv()
    product = None
    for k in range(KV_HEADS):
        for i in range(1, outers):
            peer_outer = lax.rem(outer + i, outers)
            a_copy(peer_outer, peer_outer, i, k).wait_recv()
        cols = pl.ds(k * HALF, HALF)
        rows = (
            attn[:, :, cols]
            .astype(jnp.float32)
            .reshape(outers * own, HALF)
            .astype(jnp.bfloat16)
        )
        terms = [
            lax.dot_general(
                rows,
                wbuf[j, :, cols],
                (((1,), (1,)), ((), ())),
                preferred_element_type=jnp.float32,
            )
            for j in range(INNER)
        ]
        product = terms if k == 0 else [a + b for a, b in zip(product, terms)]
    for j in range(INNER):
        yb[:, j] = product[j].reshape(outers, own, product[j].shape[1]).astype(jnp.bfloat16)

    def y_copy(row_outer, slot, peer_outer, index):
        return remote(
            yb.at[row_outer],
            yrecv.at[slot],
            y_send.at[index],
            y_recv.at[slot],
            peer_outer * INNER + inner,
        )

    for i in range(1, outers):
        peer_outer = lax.rem(outer + i, outers)
        y_copy(peer_outer, outer, peer_outer, i).start()
    yrecv[outer] = yb[outer]

    w_across.wait_send()
    w_sibling.wait_send()
    w_forward.wait_send()
    kv_copy.wait_send()

    @pl.loop(1, n)
    def _(i):
        peer = lax.rem(me + i, n)
        q_copy(peer, me, i).wait_send()
        s_copy(peer, me, peer, i).wait_send()
        n_copy(peer, me, peer, i, 0).wait_send()
        n_copy(peer, me, peer, i, 1).wait_send()

    for i in range(1, outers):
        peer_outer = lax.rem(outer + i, outers)
        a_copy(outer, peer_outer, i, 0).wait_send()
        a_copy(outer, peer_outer, i, 1).wait_send()
        y_copy(peer_outer, peer_outer, peer_outer, i).wait_recv()
    for i in range(1, outers):
        peer_outer = lax.rem(outer + i, outers)
        y_copy(peer_outer, outer, peer_outer, i).wait_send()
    pieces = [
        yrecv[o, j].astype(jnp.float32) for o in range(outers) for j in range(INNER)
    ]
    out_ref[...] = jnp.concatenate(pieces, axis=1).astype(jnp.bfloat16)


def body(visual, vis_proj, kv_proj, out_proj, queries, frame_range, text_lens):
    n = lax.axis_size("seq")
    own = queries.shape[0]
    local = visual.shape[0]
    outers = n // INNER
    cols = out_proj.shape[1]
    low = jnp.bfloat16
    dma = pltpu.SemaphoreType.DMA
    hbm = pl.BlockSpec(memory_space=pl.ANY)
    smem = pl.BlockSpec(memory_space=pltpu.SMEM)
    vmem = pl.BlockSpec(memory_space=pltpu.VMEM)
    result = pl.pallas_call(
        functools.partial(kernel, n),
        out_shape=jax.ShapeDtypeStruct((own, n * cols), low),
        in_specs=[hbm, hbm, hbm, hbm, vmem, smem, smem],
        out_specs=vmem,
        scratch_shapes=[
            pltpu.VMEM(visual.shape, low),
            pltpu.VMEM(vis_proj.shape, low),
            pltpu.VMEM(kv_proj.shape, low),
            pltpu.VMEM((INNER, cols, out_proj.shape[0]), low),
            pltpu.VMEM((local, vis_proj.shape[1]), low),
            pltpu.VMEM((2, 2, local, HEAD_DIM), low),
            pltpu.VMEM((2, local, HEAD_DIM), low),
            pltpu.VMEM((n, own, HALF), low),
            pltpu.VMEM((n, own, HALF), low),
            pltpu.VMEM((n, own, HALF), low),
            pltpu.VMEM((n, own, HEAD_DIM), jnp.float32),
            pltpu.VMEM((n, own, HEAD_DIM), jnp.float32),
            pltpu.VMEM((outers, own, HEADS * HEAD_DIM), low),
            pltpu.VMEM((outers, INNER, own, cols), low),
            pltpu.VMEM((outers, INNER, own, cols), low),
            dma((3,)),
            dma((vis_proj.shape[1] // COLS,)),
            dma((3,)),
            dma((INNER,)),
            dma,
            dma,
            dma((n,)),
            dma((n,)),
            dma((2, n)),
            dma((2, n)),
            dma((n,)),
            dma((n,)),
            dma((2, outers)),
            dma((2, outers)),
            dma((outers,)),
            dma((outers,)),
        ],
        compiler_params=pltpu.CompilerParams(
            collective_id=0, has_side_effects=True, vmem_limit_bytes=56 * 1024 * 1024
        ),
        name="layer",
    )(visual, vis_proj, kv_proj, out_proj.T, queries, frame_range, text_lens)
    return result


def solution(mesh):
    placed = (
        P(("groups", "seq"), None),
        P(),
        P(),
        P(None, "seq"),
        P(("groups", "seq"), None),
        P("groups", None),
        P("groups"),
    )
    return jax.shard_map(
        body, mesh=mesh, in_specs=placed, out_specs=P(("groups", "seq"), None), check_vma=False
    )
```

```python
import functools
import math

import jax
import jax.numpy as jnp
from jax import lax
from jax.experimental import pallas as pl
from jax.experimental.pallas import tpu as pltpu
from jax.sharding import PartitionSpec as P

HEADS = 14
KV_HEADS = 2
GROUP = HEADS // KV_HEADS
HEAD_DIM = 128
FRAME_TOK = 256
QBLK = 128
HALF = GROUP * HEAD_DIM
INNER = 4
COLS = 256
ROWS = 256
NEG = -1e30
FLOOR = -1e29
EXP_SCALE = HEAD_DIM ** (-0.5) * math.log2(math.e)
GELU_SCALE = math.sqrt(2.0 / math.pi)
GELU_CUBE = 0.044715 * GELU_SCALE
SPLIT = 4
MESH = pl.DeviceIdType.MESH


def gelu(v):
    half = 0.5 * v
    return half + half * jnp.tanh(v * (GELU_SCALE + GELU_CUBE * (v * v)))


def kernel(
    n,
    vis_hbm,
    vp_hbm,
    kvp_hbm,
    wo_hbm,
    q_ref,
    range_ref,
    lens_ref,
    out_ref,
    vis,
    vp,
    kvp,
    wbuf,
    hidden,
    kvbuf,
    kvsend,
    qbuf,
    nums,
    numrecv,
    stats,
    statrecv,
    attn,
    yb,
    yrecv,
    load_sem,
    vp_sem,
    w_send,
    w_recv,
    kv_send,
    kv_recv,
    q_send,
    q_recv,
    n_send,
    n_recv,
    s_send,
    s_recv,
    a_send,
    a_recv,
    y_send,
    y_recv,
):
    me = lax.axis_index("seq")
    core = lax.rem(me, 2)
    other = 1 - core
    sibling = me + 1 - 2 * core
    inner = lax.rem(me, INNER)
    outer = lax.div(me, INNER)
    base = me - inner
    across_slot = lax.rem(inner + 2, INNER)
    across = base + across_slot
    sibling_slot = sibling - base
    last_slot = lax.rem(sibling_slot + 2, INNER)
    outers = n // INNER
    own = q_ref.shape[0]
    local = vis.shape[0]
    width = vp.shape[1]
    starts = [0] + list(range(COLS, width, 2 * COLS))
    chunks = len(starts)
    blocks = n * own // QBLK
    per_block = QBLK // own

    vis_copy = pltpu.make_async_copy(vis_hbm, vis, load_sem.at[0])
    vis_copy.start()

    def chunk_columns(j):
        stop = starts[j + 1] if j + 1 < chunks else width
        return pl.ds(starts[j], stop - starts[j])

    def vp_copy(j):
        cols = chunk_columns(j)
        return pltpu.make_async_copy(vp_hbm.at[:, cols], vp.at[:, cols], vp_sem.at[j])

    vp_copy(0).start()
    w_copy = pltpu.make_async_copy(wo_hbm, wbuf.at[inner], load_sem.at[1])
    w_copy.start()
    for j in range(1, chunks):
        vp_copy(j).start()
    kvp_copy = pltpu.make_async_copy(kvp_hbm, kvp, load_sem.at[2])
    kvp_copy.start()

    barrier = pltpu.get_barrier_semaphore()

    @pl.loop(1, n)
    def _(i):
        pl.semaphore_signal(
            barrier, inc=1, device_id={"seq": lax.rem(me + i, n)}, device_id_type=MESH
        )

    def remote(src, dst, send, recv, peer):
        return pltpu.make_async_remote_copy(
            src_ref=src,
            dst_ref=dst,
            send_sem=send,
            recv_sem=recv,
            device_id={"seq": peer},
            device_id_type=MESH,
        )

    def hidden_chunk(j):
        vp_copy(j).wait()
        cols = chunk_columns(j)
        for r in range(local // ROWS):
            rows = pl.ds(r * ROWS, ROWS)
            value = jnp.dot(vis[rows, :], vp[:, cols], preferred_element_type=jnp.float32)
            hidden[rows, cols] = gelu(value).astype(jnp.bfloat16)

    vis_copy.wait()
    hidden_chunk(0)

    pl.semaphore_wait(barrier, n - 1)

    def q_copy(peer, slot, index):
        head = pl.ds(pl.multiple_of(lax.rem(peer, 2) * HALF, HEAD_DIM), HALF)
        return remote(q_ref.at[:, head], qbuf.at[slot], q_send.at[index], q_recv.at[slot], peer)

    @pl.loop(1, n)
    def _(i):
        q_copy(lax.rem(me + i, n), me, i).start()

    w_copy.wait()
    w_across = remote(
        wbuf.at[inner], wbuf.at[inner], w_send.at[0], w_recv.at[inner], across
    )
    w_sibling = remote(
        wbuf.at[inner], wbuf.at[inner], w_send.at[1], w_recv.at[inner], sibling
    )
    w_across.start()
    w_sibling.start()
    qbuf[me] = q_ref[:, pl.ds(pl.multiple_of(core * HALF, HEAD_DIM), HALF)]

    for j in range(1, chunks):
        hidden_chunk(j)

    kvp_copy.wait()

    def project(head, store):
        keys = pl.ds(pl.multiple_of(head * HEAD_DIM, HEAD_DIM), HEAD_DIM)
        values = pl.ds(
            pl.multiple_of((KV_HEADS + head) * HEAD_DIM, HEAD_DIM), HEAD_DIM
        )
        weights = jnp.concatenate([kvp[:, keys], kvp[:, values]], axis=1)
        for r in range(local // ROWS):
            rows = pl.ds(r * ROWS, ROWS)
            both = jnp.dot(
                hidden[rows, :], weights, preferred_element_type=jnp.float32
            ).astype(jnp.bfloat16)
            store(rows, both[:, :HEAD_DIM], both[:, HEAD_DIM:])

    def store_send(rows, keys, values):
        kvsend[0, rows, :] = keys
        kvsend[1, rows, :] = values

    def store_own(rows, keys, values):
        kvbuf[0, 0, rows, :] = keys
        kvbuf[0, 1, rows, :] = values

    project(other, store_send)
    kv_copy = remote(kvsend, kvbuf.at[1], kv_send, kv_recv, sibling)
    kv_copy.start()
    project(core, store_own)

    def w_arrival(slot):
        return remote(wbuf.at[slot], wbuf.at[slot], w_send.at[2], w_recv.at[slot], sibling)

    @pl.loop(1, n)
    def _(i):
        peer = lax.rem(me + i, n)
        q_copy(peer, peer, i).wait_recv()

    kv_copy.wait_recv()

    lane = lax.broadcasted_iota(jnp.int32, (QBLK, HEAD_DIM), 1)
    token = lax.broadcasted_iota(jnp.int32, (1, local), 1)
    def n_copy(row_owner, slot, peer, index, part):
        cols = pl.ds(0, SPLIT * HEAD_DIM) if part == 0 else pl.ds(SPLIT * HEAD_DIM, HALF - SPLIT * HEAD_DIM)
        return remote(
            nums.at[row_owner, :, cols],
            numrecv.at[slot, :, cols],
            n_send.at[part, index],
            n_recv.at[part, slot],
            peer,
        )

    def s_copy(row_owner, slot, peer, index):
        return remote(
            stats.at[row_owner], statrecv.at[slot], s_send.at[index], s_recv.at[slot], peer
        )

    allowed = []
    for b in range(blocks):
        low = range_ref[b, 0] * FRAME_TOK
        high = range_ref[b, 1] * FRAME_TOK
        for device in (me, sibling):
            row = token + device * local
            allowed.append((row >= low) & (row < high))
    stat = [jnp.zeros((QBLK, HEAD_DIM), jnp.float32)] * blocks
    for h in range(GROUP):
        cols = pl.ds(h * HEAD_DIM, HEAD_DIM)
        for b in range(blocks):
            owners = pl.ds(b * per_block, per_block)
            query = (
                qbuf[owners, :, cols]
                .astype(jnp.float32)
                .reshape(QBLK, HEAD_DIM)
                .astype(jnp.bfloat16)
            )
            scores = []
            for slot in range(2):
                raw = lax.dot_general(
                    query,
                    kvbuf[slot, 0],
                    (((1,), (1,)), ((), ())),
                    preferred_element_type=jnp.float32,
                )
                scores.append(jnp.where(allowed[2 * b + slot], raw, NEG))
            top = jnp.maximum(
                jnp.max(jnp.maximum(scores[0], scores[1]), axis=1, keepdims=True), FLOOR
            )
            weights = [jnp.exp2((s - top) * EXP_SCALE) for s in scores]
            total = jnp.sum(weights[0] + weights[1], axis=1, keepdims=True)
            numer = jnp.dot(
                weights[0].astype(jnp.bfloat16),
                kvbuf[0, 1],
                preferred_element_type=jnp.float32,
            ) + jnp.dot(
                weights[1].astype(jnp.bfloat16),
                kvbuf[1, 1],
                preferred_element_type=jnp.float32,
            )
            nums[owners, :, cols] = numer.reshape(per_block, own, HEAD_DIM).astype(
                jnp.bfloat16
            )
            stat[b] = jnp.where(lane == h, top, stat[b])
            stat[b] = jnp.where(lane == h + HEAD_DIM // 2, total, stat[b])
        if h == SPLIT - 1:

            @pl.loop(1, n)
            def _(i):
                peer = lax.rem(me + i, n)
                n_copy(peer, me, peer, i, 0).start()

    for b in range(blocks):
        stats[pl.ds(b * per_block, per_block)] = stat[b].reshape(per_block, own, HEAD_DIM)

    @pl.loop(1, n)
    def _(i):
        peer = lax.rem(me + i, n)
        s_copy(peer, me, peer, i).start()
        n_copy(peer, me, peer, i, 1).start()

    w_arrival(across_slot).wait_recv()
    w_forward = w_arrival(across_slot)
    w_forward.start()

    numrecv[me] = nums[me]
    statrecv[me] = stats[me]

    @pl.loop(1, n)
    def _(i):
        peer = lax.rem(me + i, n)
        s_copy(peer, peer, peer, i).wait_recv()

    length = lens_ref[lax.div(me * own, QBLK)]
    position = lax.rem(me * own, QBLK) + lax.broadcasted_iota(jnp.int32, (own, HEAD_DIM), 0)
    valid = position < length
    parts = (range(SPLIT), range(SPLIT, GROUP))

    def piece_columns(piece):
        heads = parts[piece // KV_HEADS]
        start = (piece % KV_HEADS) * HALF + heads[0] * HEAD_DIM
        return pl.ds(start, len(heads) * HEAD_DIM)

    def a_copy(slot, peer_outer, index, part):
        cols = piece_columns(part)
        return remote(
            attn.at[slot, :, cols],
            attn.at[slot, :, cols],
            a_send.at[part, index],
            a_recv.at[part, slot],
            peer_outer * INNER + inner,
        )

    scaled = []
    for k in range(KV_HEADS):
        sources = range(k, n, KV_HEADS)
        top = functools.reduce(jnp.maximum, [statrecv[s] for s in sources])
        factors = [jnp.exp2((statrecv[s] - top) * EXP_SCALE) for s in sources]
        totals = functools.reduce(
            jnp.add,
            [
                f * pltpu.roll(statrecv[s], HEAD_DIM // 2, 1)
                for f, s in zip(factors, sources)
            ],
        )
        scaled.append((factors, totals))

    for part, heads in enumerate(parts):

        @pl.loop(1, n)
        def _(i):
            peer = lax.rem(me + i, n)
            n_copy(peer, peer, peer, i, part).wait_recv()

        for k in range(KV_HEADS):
            factors, totals = scaled[k]
            for h in heads:
                cols = pl.ds(h * HEAD_DIM, HEAD_DIM)
                sums = functools.reduce(
                    jnp.add,
                    [
                        numrecv[s, :, cols].astype(jnp.float32) * f[:, h : h + 1]
                        for f, s in zip(factors, range(k, n, KV_HEADS))
                    ],
                )
                normed = jnp.where(valid, sums / totals[:, h : h + 1], 0.0)
                attn[outer, :, pl.ds(k * HALF + h * HEAD_DIM, HEAD_DIM)] = normed.astype(
                    jnp.bfloat16
                )
            for i in range(1, outers):
                a_copy(outer, lax.rem(outer + i, outers), i, part * KV_HEADS + k).start()

    w_arrival(sibling_slot).wait_recv()
    w_arrival(last_slot).wait_recv()
    product = None
    for k in range(2 * KV_HEADS):
        for i in range(1, outers):
            peer_outer = lax.rem(outer + i, outers)
            a_copy(peer_outer, peer_outer, i, k).wait_recv()
        cols = piece_columns(k)
        rows = (
            attn[:, :, cols]
            .astype(jnp.float32)
            .reshape(outers * own, cols.size)
            .astype(jnp.bfloat16)
        )
        terms = [
            lax.dot_general(
                rows,
                wbuf[j, :, cols],
                (((1,), (1,)), ((), ())),
                preferred_element_type=jnp.float32,
            )
            for j in range(INNER)
        ]
        product = terms if k == 0 else [a + b for a, b in zip(product, terms)]
    for j in range(INNER):
        yb[:, j] = product[j].reshape(outers, own, product[j].shape[1]).astype(jnp.bfloat16)

    def y_copy(row_outer, slot, peer_outer, index):
        return remote(
            yb.at[row_outer],
            yrecv.at[slot],
            y_send.at[index],
            y_recv.at[slot],
            peer_outer * INNER + inner,
        )

    for i in range(1, outers):
        peer_outer = lax.rem(outer + i, outers)
        y_copy(peer_outer, outer, peer_outer, i).start()
    yrecv[outer] = yb[outer]

    w_across.wait_send()
    w_sibling.wait_send()
    w_forward.wait_send()
    kv_copy.wait_send()

    @pl.loop(1, n)
    def _(i):
        peer = lax.rem(me + i, n)
        q_copy(peer, me, i).wait_send()
        s_copy(peer, me, peer, i).wait_send()
        n_copy(peer, me, peer, i, 0).wait_send()
        n_copy(peer, me, peer, i, 1).wait_send()

    for i in range(1, outers):
        peer_outer = lax.rem(outer + i, outers)
        for k in range(2 * KV_HEADS):
            a_copy(outer, peer_outer, i, k).wait_send()
        y_copy(peer_outer, peer_outer, peer_outer, i).wait_recv()
    for i in range(1, outers):
        peer_outer = lax.rem(outer + i, outers)
        y_copy(peer_outer, outer, peer_outer, i).wait_send()
    pieces = [
        yrecv[o, j].astype(jnp.float32) for o in range(outers) for j in range(INNER)
    ]
    out_ref[...] = jnp.concatenate(pieces, axis=1).astype(jnp.bfloat16)


def body(visual, vis_proj, kv_proj, out_proj, queries, frame_range, text_lens):
    n = lax.axis_size("seq")
    own = queries.shape[0]
    local = visual.shape[0]
    outers = n // INNER
    cols = out_proj.shape[1]
    low = jnp.bfloat16
    dma = pltpu.SemaphoreType.DMA
    hbm = pl.BlockSpec(memory_space=pl.ANY)
    smem = pl.BlockSpec(memory_space=pltpu.SMEM)
    vmem = pl.BlockSpec(memory_space=pltpu.VMEM)
    result = pl.pallas_call(
        functools.partial(kernel, n),
        out_shape=jax.ShapeDtypeStruct((own, n * cols), low),
        in_specs=[hbm, hbm, hbm, hbm, vmem, smem, smem],
        out_specs=vmem,
        scratch_shapes=[
            pltpu.VMEM(visual.shape, low),
            pltpu.VMEM(vis_proj.shape, low),
            pltpu.VMEM(kv_proj.shape, low),
            pltpu.VMEM((INNER, cols, out_proj.shape[0]), low),
            pltpu.VMEM((local, vis_proj.shape[1]), low),
            pltpu.VMEM((2, 2, local, HEAD_DIM), low),
            pltpu.VMEM((2, local, HEAD_DIM), low),
            pltpu.VMEM((n, own, HALF), low),
            pltpu.VMEM((n, own, HALF), low),
            pltpu.VMEM((n, own, HALF), low),
            pltpu.VMEM((n, own, HEAD_DIM), jnp.float32),
            pltpu.VMEM((n, own, HEAD_DIM), jnp.float32),
            pltpu.VMEM((outers, own, HEADS * HEAD_DIM), low),
            pltpu.VMEM((outers, INNER, own, cols), low),
            pltpu.VMEM((outers, INNER, own, cols), low),
            dma((3,)),
            dma((vis_proj.shape[1] // COLS,)),
            dma((3,)),
            dma((INNER,)),
            dma,
            dma,
            dma((n,)),
            dma((n,)),
            dma((2, n)),
            dma((2, n)),
            dma((n,)),
            dma((n,)),
            dma((2 * KV_HEADS, outers)),
            dma((2 * KV_HEADS, outers)),
            dma((outers,)),
            dma((outers,)),
        ],
        compiler_params=pltpu.CompilerParams(
            collective_id=0, has_side_effects=True, vmem_limit_bytes=56 * 1024 * 1024
        ),
        name="layer",
    )(visual, vis_proj, kv_proj, out_proj.T, queries, frame_range, text_lens)
    return result


def solution(mesh):
    placed = (
        P(("groups", "seq"), None),
        P(),
        P(),
        P(None, "seq"),
        P(("groups", "seq"), None),
        P("groups", None),
        P("groups"),
    )
    return jax.shard_map(
        body, mesh=mesh, in_specs=placed, out_specs=P(("groups", "seq"), None), check_vma=False
    )
```

```python
import functools
import math

import jax
import jax.numpy as jnp
from jax import lax
from jax.experimental import pallas as pl
from jax.experimental.pallas import tpu as pltpu
from jax.sharding import PartitionSpec as P

HEADS = 14
KV_HEADS = 2
GROUP = HEADS // KV_HEADS
HEAD_DIM = 128
FRAME_TOK = 256
QBLK = 128
HALF = GROUP * HEAD_DIM
INNER = 4
COLS = 256
ROWS = 256
NEG = -1e30
FLOOR = -1e29
EXP_SCALE = HEAD_DIM ** (-0.5) * math.log2(math.e)
GELU_SCALE = math.sqrt(2.0 / math.pi)
GELU_CUBE = 0.044715 * GELU_SCALE
SPLIT = 3
MESH = pl.DeviceIdType.MESH


def gelu(v):
    half = 0.5 * v
    return half + half * jnp.tanh(v * (GELU_SCALE + GELU_CUBE * (v * v)))


def kernel(
    n,
    vis_hbm,
    vp_hbm,
    kvp_hbm,
    wo_hbm,
    q_ref,
    range_ref,
    lens_ref,
    out_ref,
    vis,
    vp,
    kvp,
    wbuf,
    hidden,
    kvbuf,
    kvsend,
    qbuf,
    nums,
    numrecv,
    stats,
    statrecv,
    attn,
    yb,
    yrecv,
    load_sem,
    vp_sem,
    w_send,
    w_recv,
    kv_send,
    kv_recv,
    q_send,
    q_recv,
    n_send,
    n_recv,
    s_send,
    s_recv,
    a_send,
    a_recv,
    y_send,
    y_recv,
):
    me = lax.axis_index("seq")
    core = lax.rem(me, 2)
    other = 1 - core
    sibling = me + 1 - 2 * core
    inner = lax.rem(me, INNER)
    outer = lax.div(me, INNER)
    base = me - inner
    across_slot = lax.rem(inner + 2, INNER)
    across = base + across_slot
    sibling_slot = sibling - base
    last_slot = lax.rem(sibling_slot + 2, INNER)
    outers = n // INNER
    own = q_ref.shape[0]
    local = vis.shape[0]
    width = vp.shape[1]
    starts = [0] + list(range(COLS, width, 2 * COLS))
    chunks = len(starts)
    blocks = n * own // QBLK
    per_block = QBLK // own

    vis_copy = pltpu.make_async_copy(vis_hbm, vis, load_sem.at[0])
    vis_copy.start()

    def chunk_columns(j):
        stop = starts[j + 1] if j + 1 < chunks else width
        return pl.ds(starts[j], stop - starts[j])

    def vp_copy(j):
        cols = chunk_columns(j)
        return pltpu.make_async_copy(vp_hbm.at[:, cols], vp.at[:, cols], vp_sem.at[j])

    vp_copy(0).start()
    w_copy = pltpu.make_async_copy(wo_hbm, wbuf.at[inner], load_sem.at[1])
    w_copy.start()
    for j in range(1, chunks):
        vp_copy(j).start()
    kvp_copy = pltpu.make_async_copy(kvp_hbm, kvp, load_sem.at[2])
    kvp_copy.start()

    barrier = pltpu.get_barrier_semaphore()

    @pl.loop(1, n)
    def _(i):
        pl.semaphore_signal(
            barrier, inc=1, device_id={"seq": lax.rem(me + i, n)}, device_id_type=MESH
        )

    def remote(src, dst, send, recv, peer):
        return pltpu.make_async_remote_copy(
            src_ref=src,
            dst_ref=dst,
            send_sem=send,
            recv_sem=recv,
            device_id={"seq": peer},
            device_id_type=MESH,
        )

    def hidden_chunk(j):
        vp_copy(j).wait()
        cols = chunk_columns(j)
        for r in range(local // ROWS):
            rows = pl.ds(r * ROWS, ROWS)
            value = jnp.dot(vis[rows, :], vp[:, cols], preferred_element_type=jnp.float32)
            hidden[rows, cols] = gelu(value).astype(jnp.bfloat16)

    vis_copy.wait()
    hidden_chunk(0)

    pl.semaphore_wait(barrier, n - 1)

    def q_copy(peer, slot, index):
        head = pl.ds(pl.multiple_of(lax.rem(peer, 2) * HALF, HEAD_DIM), HALF)
        return remote(q_ref.at[:, head], qbuf.at[slot], q_send.at[index], q_recv.at[slot], peer)

    @pl.loop(1, n)
    def _(i):
        q_copy(lax.rem(me + i, n), me, i).start()

    w_copy.wait()
    w_across = remote(
        wbuf.at[inner], wbuf.at[inner], w_send.at[0], w_recv.at[inner], across
    )
    w_sibling = remote(
        wbuf.at[inner], wbuf.at[inner], w_send.at[1], w_recv.at[inner], sibling
    )
    w_across.start()
    w_sibling.start()
    qbuf[me] = q_ref[:, pl.ds(pl.multiple_of(core * HALF, HEAD_DIM), HALF)]

    for j in range(1, chunks):
        hidden_chunk(j)

    kvp_copy.wait()

    def project(head, store):
        keys = pl.ds(pl.multiple_of(head * HEAD_DIM, HEAD_DIM), HEAD_DIM)
        values = pl.ds(
            pl.multiple_of((KV_HEADS + head) * HEAD_DIM, HEAD_DIM), HEAD_DIM
        )
        weights = jnp.concatenate([kvp[:, keys], kvp[:, values]], axis=1)
        for r in range(local // ROWS):
            rows = pl.ds(r * ROWS, ROWS)
            both = jnp.dot(
                hidden[rows, :], weights, preferred_element_type=jnp.float32
            ).astype(jnp.bfloat16)
            store(rows, both[:, :HEAD_DIM], both[:, HEAD_DIM:])

    def store_send(rows, keys, values):
        kvsend[0, rows, :] = keys
        kvsend[1, rows, :] = values

    def store_own(rows, keys, values):
        kvbuf[0, 0, rows, :] = keys
        kvbuf[0, 1, rows, :] = values

    project(other, store_send)
    kv_copy = remote(kvsend, kvbuf.at[1], kv_send, kv_recv, sibling)
    kv_copy.start()
    project(core, store_own)

    def w_arrival(slot):
        return remote(wbuf.at[slot], wbuf.at[slot], w_send.at[2], w_recv.at[slot], sibling)

    @pl.loop(1, n)
    def _(i):
        peer = lax.rem(me + i, n)
        q_copy(peer, peer, i).wait_recv()

    kv_copy.wait_recv()

    lane = lax.broadcasted_iota(jnp.int32, (QBLK, HEAD_DIM), 1)
    token = lax.broadcasted_iota(jnp.int32, (1, local), 1)
    def n_copy(row_owner, slot, peer, index, part):
        cols = pl.ds(0, SPLIT * HEAD_DIM) if part == 0 else pl.ds(SPLIT * HEAD_DIM, HALF - SPLIT * HEAD_DIM)
        return remote(
            nums.at[row_owner, :, cols],
            numrecv.at[slot, :, cols],
            n_send.at[part, index],
            n_recv.at[part, slot],
            peer,
        )

    def s_copy(row_owner, slot, peer, index):
        return remote(
            stats.at[row_owner], statrecv.at[slot], s_send.at[index], s_recv.at[slot], peer
        )

    allowed = []
    for b in range(blocks):
        low = range_ref[b, 0] * FRAME_TOK
        high = range_ref[b, 1] * FRAME_TOK
        for device in (me, sibling):
            row = token + device * local
            allowed.append((row >= low) & (row < high))
    stat = [jnp.zeros((QBLK, HEAD_DIM), jnp.float32)] * blocks
    for h in range(GROUP):
        cols = pl.ds(h * HEAD_DIM, HEAD_DIM)
        for b in range(blocks):
            owners = pl.ds(b * per_block, per_block)
            query = (
                qbuf[owners, :, cols]
                .astype(jnp.float32)
                .reshape(QBLK, HEAD_DIM)
                .astype(jnp.bfloat16)
            )
            scores = []
            for slot in range(2):
                raw = lax.dot_general(
                    query,
                    kvbuf[slot, 0],
                    (((1,), (1,)), ((), ())),
                    preferred_element_type=jnp.float32,
                )
                scores.append(jnp.where(allowed[2 * b + slot], raw, NEG))
            top = jnp.maximum(
                jnp.max(jnp.maximum(scores[0], scores[1]), axis=1, keepdims=True), FLOOR
            )
            weights = [jnp.exp2((s - top) * EXP_SCALE) for s in scores]
            total = jnp.sum(weights[0] + weights[1], axis=1, keepdims=True)
            numer = jnp.dot(
                weights[0].astype(jnp.bfloat16),
                kvbuf[0, 1],
                preferred_element_type=jnp.float32,
            ) + jnp.dot(
                weights[1].astype(jnp.bfloat16),
                kvbuf[1, 1],
                preferred_element_type=jnp.float32,
            )
            nums[owners, :, cols] = numer.reshape(per_block, own, HEAD_DIM).astype(
                jnp.bfloat16
            )
            stat[b] = jnp.where(lane == h, top, stat[b])
            stat[b] = jnp.where(lane == h + HEAD_DIM // 2, total, stat[b])
        if h == SPLIT - 1:

            @pl.loop(1, n)
            def _(i):
                peer = lax.rem(me + i, n)
                n_copy(peer, me, peer, i, 0).start()

    for b in range(blocks):
        stats[pl.ds(b * per_block, per_block)] = stat[b].reshape(per_block, own, HEAD_DIM)

    @pl.loop(1, n)
    def _(i):
        peer = lax.rem(me + i, n)
        s_copy(peer, me, peer, i).start()
        n_copy(peer, me, peer, i, 1).start()

    w_arrival(across_slot).wait_recv()
    w_forward = w_arrival(across_slot)
    w_forward.start()

    numrecv[me] = nums[me]
    statrecv[me] = stats[me]

    @pl.loop(1, n)
    def _(i):
        peer = lax.rem(me + i, n)
        s_copy(peer, peer, peer, i).wait_recv()

    length = lens_ref[lax.div(me * own, QBLK)]
    position = lax.rem(me * own, QBLK) + lax.broadcasted_iota(jnp.int32, (own, HEAD_DIM), 0)
    valid = position < length
    parts = (range(SPLIT), range(SPLIT, GROUP))

    def piece_columns(piece):
        heads = parts[piece // KV_HEADS]
        start = (piece % KV_HEADS) * HALF + heads[0] * HEAD_DIM
        return pl.ds(start, len(heads) * HEAD_DIM)

    def a_copy(slot, peer_outer, index, part):
        cols = piece_columns(part)
        return remote(
            attn.at[slot, :, cols],
            attn.at[slot, :, cols],
            a_send.at[part, index],
            a_recv.at[part, slot],
            peer_outer * INNER + inner,
        )

    scaled = []
    for k in range(KV_HEADS):
        sources = range(k, n, KV_HEADS)
        top = functools.reduce(jnp.maximum, [statrecv[s] for s in sources])
        factors = [jnp.exp2((statrecv[s] - top) * EXP_SCALE) for s in sources]
        totals = functools.reduce(
            jnp.add,
            [
                f * pltpu.roll(statrecv[s], HEAD_DIM // 2, 1)
                for f, s in zip(factors, sources)
            ],
        )
        scaled.append((factors, totals))

    for part, heads in enumerate(parts):

        @pl.loop(1, n)
        def _(i):
            peer = lax.rem(me + i, n)
            n_copy(peer, peer, peer, i, part).wait_recv()

        for k in range(KV_HEADS):
            factors, totals = scaled[k]
            for h in heads:
                cols = pl.ds(h * HEAD_DIM, HEAD_DIM)
                sums = functools.reduce(
                    jnp.add,
                    [
                        numrecv[s, :, cols].astype(jnp.float32) * f[:, h : h + 1]
                        for f, s in zip(factors, range(k, n, KV_HEADS))
                    ],
                )
                normed = jnp.where(valid, sums / totals[:, h : h + 1], 0.0)
                attn[outer, :, pl.ds(k * HALF + h * HEAD_DIM, HEAD_DIM)] = normed.astype(
                    jnp.bfloat16
                )
            for i in range(1, outers):
                a_copy(outer, lax.rem(outer + i, outers), i, part * KV_HEADS + k).start()

    w_arrival(sibling_slot).wait_recv()
    w_arrival(last_slot).wait_recv()
    product = None
    for k in range(2 * KV_HEADS):
        for i in range(1, outers):
            peer_outer = lax.rem(outer + i, outers)
            a_copy(peer_outer, peer_outer, i, k).wait_recv()
        cols = piece_columns(k)
        rows = (
            attn[:, :, cols]
            .astype(jnp.float32)
            .reshape(outers * own, cols.size)
            .astype(jnp.bfloat16)
        )
        terms = [
            lax.dot_general(
                rows,
                wbuf[j, :, cols],
                (((1,), (1,)), ((), ())),
                preferred_element_type=jnp.float32,
            )
            for j in range(INNER)
        ]
        product = terms if k == 0 else [a + b for a, b in zip(product, terms)]
    for j in range(INNER):
        yb[:, j] = product[j].reshape(outers, own, product[j].shape[1]).astype(jnp.bfloat16)

    def y_copy(row_outer, slot, peer_outer, index):
        return remote(
            yb.at[row_outer],
            yrecv.at[slot],
            y_send.at[index],
            y_recv.at[slot],
            peer_outer * INNER + inner,
        )

    for i in range(1, outers):
        peer_outer = lax.rem(outer + i, outers)
        y_copy(peer_outer, outer, peer_outer, i).start()
    yrecv[outer] = yb[outer]

    w_across.wait_send()
    w_sibling.wait_send()
    w_forward.wait_send()
    kv_copy.wait_send()

    @pl.loop(1, n)
    def _(i):
        peer = lax.rem(me + i, n)
        q_copy(peer, me, i).wait_send()
        s_copy(peer, me, peer, i).wait_send()
        n_copy(peer, me, peer, i, 0).wait_send()
        n_copy(peer, me, peer, i, 1).wait_send()

    for i in range(1, outers):
        peer_outer = lax.rem(outer + i, outers)
        for k in range(2 * KV_HEADS):
            a_copy(outer, peer_outer, i, k).wait_send()
        y_copy(peer_outer, peer_outer, peer_outer, i).wait_recv()
    for i in range(1, outers):
        peer_outer = lax.rem(outer + i, outers)
        y_copy(peer_outer, outer, peer_outer, i).wait_send()
    pieces = [
        yrecv[o, j].astype(jnp.float32) for o in range(outers) for j in range(INNER)
    ]
    out_ref[...] = jnp.concatenate(pieces, axis=1).astype(jnp.bfloat16)


def body(visual, vis_proj, kv_proj, out_proj, queries, frame_range, text_lens):
    n = lax.axis_size("seq")
    own = queries.shape[0]
    local = visual.shape[0]
    outers = n // INNER
    cols = out_proj.shape[1]
    low = jnp.bfloat16
    dma = pltpu.SemaphoreType.DMA
    hbm = pl.BlockSpec(memory_space=pl.ANY)
    smem = pl.BlockSpec(memory_space=pltpu.SMEM)
    vmem = pl.BlockSpec(memory_space=pltpu.VMEM)
    result = pl.pallas_call(
        functools.partial(kernel, n),
        out_shape=jax.ShapeDtypeStruct((own, n * cols), low),
        in_specs=[hbm, hbm, hbm, hbm, vmem, smem, smem],
        out_specs=vmem,
        scratch_shapes=[
            pltpu.VMEM(visual.shape, low),
            pltpu.VMEM(vis_proj.shape, low),
            pltpu.VMEM(kv_proj.shape, low),
            pltpu.VMEM((INNER, cols, out_proj.shape[0]), low),
            pltpu.VMEM((local, vis_proj.shape[1]), low),
            pltpu.VMEM((2, 2, local, HEAD_DIM), low),
            pltpu.VMEM((2, local, HEAD_DIM), low),
            pltpu.VMEM((n, own, HALF), low),
            pltpu.VMEM((n, own, HALF), low),
            pltpu.VMEM((n, own, HALF), low),
            pltpu.VMEM((n, own, HEAD_DIM), jnp.float32),
            pltpu.VMEM((n, own, HEAD_DIM), jnp.float32),
            pltpu.VMEM((outers, own, HEADS * HEAD_DIM), low),
            pltpu.VMEM((outers, INNER, own, cols), low),
            pltpu.VMEM((outers, INNER, own, cols), low),
            dma((3,)),
            dma((vis_proj.shape[1] // COLS,)),
            dma((3,)),
            dma((INNER,)),
            dma,
            dma,
            dma((n,)),
            dma((n,)),
            dma((2, n)),
            dma((2, n)),
            dma((n,)),
            dma((n,)),
            dma((2 * KV_HEADS, outers)),
            dma((2 * KV_HEADS, outers)),
            dma((outers,)),
            dma((outers,)),
        ],
        compiler_params=pltpu.CompilerParams(
            collective_id=0, has_side_effects=True, vmem_limit_bytes=56 * 1024 * 1024
        ),
        name="layer",
    )(visual, vis_proj, kv_proj, out_proj.T, queries, frame_range, text_lens)
    return result


def solution(mesh):
    placed = (
        P(("groups", "seq"), None),
        P(),
        P(),
        P(None, "seq"),
        P(("groups", "seq"), None),
        P("groups", None),
        P("groups"),
    )
    return jax.shard_map(
        body, mesh=mesh, in_specs=placed, out_specs=P(("groups", "seq"), None), check_vma=False
    )
```
